512 devices in a mesh: tm: 64 (over y_hi, z, core), lat: 8 (over x, y_lo).
Axes of the slice: x: 4, y: 4 (y_hi: 2, y_lo: 2; y = y_hi * 2 + y_lo), z: 16, core: 2. Of those that a mesh axis runs over, the one named last changes fastest.
Arguments:
- fields: bfloat16 [128, 720, 1440], P('tm', 'lat'), may hold values from -6 to 6
- legendre: bfloat16 [720, 8192], P('lat'), may hold values from -0.21875 to 0.21875
- order_table: int32 [3, 16384], replicated, may hold values from 0 to 720, as said below
- window_start: int32 [1], replicated, may hold values from 0 to 8192
- ridge: float32 [1], replicated, may hold values from 0.3 to 1
Outputs:
- factored: float32 [8192, 8192], P('tm', 'lat')
The draws below stay inside these ranges and needn't reach their ends.
Inputs may be any that keep to these rules, and one draw needn't show every extreme that they name: `order_table`: row 0 holds each entry's degree, row 1 its order, which is at most the degree and below 720, row 2 is 0 for a cosine and 1 for a sine part, and is 1 only where the order is positive.
All inputs are finite; a program needn't handle non-finite values.
Results may differ from the reference program's by a relative error of at most 0.0048.
Values may be sent and summed in bfloat16 or wider, within the bound.
A program may use at most 64 MiB of HBM per device.

```python
import math
import jax
import jax.numpy as jnp
from jax import lax

T_DEV = 2
NLAT = 720
NLON = 1440
MORD = 720
LMAX = 720
K = 8192
PANEL = 512
NT = 128
TAB = 16384
N_TM = 64


def draw_order_table(key, part):
    key_order, key_degree, key_sine, key_spot = jax.random.split(jax.random.fold_in(key, 11), 4)
    position = jnp.arange(TAB, dtype=jnp.int32)
    spot_index = jax.random.randint(key_spot, (), 0, TAB)
    order_row = jax.random.randint(key_order, (TAB,), 0, MORD)
    order_row = jnp.where(position == spot_index, 0, order_row)
    extra = jax.random.randint(key_degree, (TAB,), 0, 1 << 20) % (LMAX + 1 - order_row)
    degree_row = jnp.where(position == spot_index, LMAX, order_row + extra)
    sine_row = jax.random.randint(key_sine, (TAB,), 0, 2) * (order_row > 0).astype(jnp.int32)
    return jnp.stack([degree_row, order_row, sine_row]).astype(jnp.int32)


def shard_levels(rng, extent, cuts, smallest, largest):
    loudness, own = 1.0, jax.random.fold_in(rng, 6)
    for dim, shards_of in cuts:
        steps = jnp.exp(jax.random.uniform(jax.random.fold_in(own, dim), (shards_of,), jnp.float32, smallest / len(cuts), largest / len(cuts)))
        loudness = loudness * jnp.repeat(steps, extent[dim] // shards_of).reshape([-1 if axis == dim else 1 for axis in range(len(extent))])
    return loudness


def scatter_about(stream_key, dims, deviation, most, shards=(), kind=jnp.bfloat16):
    values = jax.random.normal(stream_key, dims, jnp.float32) * deviation
    if len(shards) > 0:
        values = shard_levels(stream_key, dims, shards, -0.22, 0.18) * values
    return jnp.clip(values, min=-most, max=most).astype(kind)


def setup_inputs(seed: int = 0) -> dict:
    keys = jax.random.split(jax.random.key(seed), 6)
    fields = scatter_about(keys[0], (NT, NLAT, NLON), 1.0, 6.0, ((0, 64), (1, 8)))
    legendre = scatter_about(keys[1], (NLAT, K), NLAT ** -0.5, 0.21875, ((0, 8),))
    order_table = draw_order_table(jax.random.fold_in(keys[5], 71), 0)
    window_start = jax.random.randint(keys[3], (1,), 0, TAB - K + 1).astype(jnp.int32)
    ridge = jnp.clip(jnp.exp(jax.random.uniform(keys[4], (1,), jnp.float32, math.log(0.3), math.log(1.0))), 0.3, 1.0)
    return {"fields": fields, "legendre": legendre, "order_table": order_table, "window_start": window_start, "ridge": ridge}


def make_basis(nlon):
    half = nlon // 2
    longitude = jnp.arange(nlon, dtype=jnp.int32)[:, None]
    column = jnp.arange(nlon, dtype=jnp.int32)[None, :]
    freq = column % half
    phase = (freq * longitude % nlon).astype(jnp.float32) * (2.0 * math.pi / nlon)
    return jnp.where(column < half, jnp.cos(phase), jnp.sin(phase)).astype(jnp.bfloat16)

def legendre_contract(spectra, legendre, column):
    kcoef = legendre.shape[1]
    width = kcoef // 8

    def one_part(number):
        start = (number * width).astype(jnp.int32)
        chosen_cols = lax.dynamic_slice_in_dim(column, start, width, 0)
        weights = lax.dynamic_slice_in_dim(legendre, start, width, 1).astype(jnp.float32)
        chosen = jnp.take(spectra, chosen_cols, axis=2)
        return jnp.einsum('tlk,lk->tk', chosen, weights)
    parts_out = lax.map(one_part, jnp.arange(8, dtype=jnp.int32))
    return jnp.transpose(parts_out, (1, 0, 2)).reshape(spectra.shape[0], kcoef)

def gram_dot(left, right):
    return lax.dot_general(left.astype(jnp.float32), right.astype(jnp.float32), (((0,), (0,)), ((), ())), preferred_element_type=jnp.float32)

def reference(fields, legendre, order_table, window_start, ridge):
    window = lax.dynamic_slice_in_dim(order_table, window_start[0].astype(jnp.int32), K, 1)
    degree = window[0]
    column = (window[1] + MORD * window[2]).astype(jnp.int32)
    dft_basis = make_basis(NLON)
    scale = 1.0 / math.sqrt(NLON)

    def one_block(time_block):
        flat = time_block.reshape(T_DEV * NLAT, NLON)
        spectra = (jnp.dot(flat.astype(jnp.float32), dft_basis.astype(jnp.float32), preferred_element_type=jnp.float32) * scale).reshape(T_DEV, NLAT, NLON)
        return legendre_contract(spectra, legendre, column)
    blocks = fields.reshape(N_TM, T_DEV, NLAT, NLON)
    coeffs = lax.map(one_block, blocks).reshape(NT, K).astype(jnp.bfloat16)
    ridge_diag = ridge[0] * (1.0 + (degree * (degree + 1)).astype(jnp.float32) / float(LMAX * (LMAX + 1)))
    gram = gram_dot(coeffs, coeffs) * (1.0 / NT) + jnp.diag(ridge_diag)
    factor = jnp.linalg.cholesky(gram[:PANEL, :PANEL])
    panel = jax.scipy.linalg.solve_triangular(factor, gram[:, :PANEL].T, lower=True).T
    lower_rows = panel[PANEL:]
    schur = gram[PANEL:, PANEL:] - jnp.dot(lower_rows, lower_rows.T, precision=lax.Precision.HIGHEST)
    upper_part = jnp.concatenate([panel[:PANEL], lower_rows.T], axis=1)
    lower_part = jnp.concatenate([lower_rows, schur], axis=1)
    return jnp.concatenate([upper_part, lower_part], axis=0)
```

```python
import math

import jax
import jax.numpy as jnp
import numpy as np
from jax import lax
from jax.experimental import pallas as pl
from jax.experimental.pallas import tpu as pltpu
from jax.sharding import PartitionSpec as P

NLON = 1440
HALF = NLON // 2
LMAX = 720
NT = 128
PANEL = 512
BLOCK = 128
WIDTH = 1024
SENT = WIDTH + PANEL
LAT = 90
LATPAD = 96
DEEP = 768
CHUNK = 256
F32 = jnp.float32
BF16 = jnp.bfloat16


def half_basis():
    n = np.arange(HALF)[:, None]
    c = np.arange(HALF)[None, :]
    phase = ((n * c) % NLON).astype(np.float32) * np.float32(2.0 * math.pi / NLON)
    basis = np.zeros((2, HALF, DEEP), np.float32)
    basis[0, :, :HALF] = np.cos(phase)
    basis[1, :, :HALF] = np.sin(phase)
    return basis.astype(BF16)


def spectral_kernel(fields_ref, basis_ref, leg_ref, win_ref, out_ref, rows):
    @pl.when(pl.program_id(0) == 0)
    def _():
        lane = lax.broadcasted_iota(jnp.int32, (1, DEEP), 1)
        sign = jnp.where(lane % 2 == 0, 1.0, -1.0).astype(F32)
        for t in range(2):
            low, high = fields_ref[t, :, :HALF], fields_ref[t, :, HALF:]
            for p in range(2):
                basis = basis_ref[p]
                first = jnp.dot(low, basis, preferred_element_type=F32)
                second = jnp.dot(high, basis, preferred_element_type=F32)
                at = (2 * p + t) * LATPAD
                rows[at : at + LAT, :] = (first + sign * second).astype(BF16)

    iota = lax.broadcasted_iota(jnp.int32, (CHUNK, CHUNK), 0).astype(F32).astype(BF16)
    one, zero = jnp.ones((CHUNK, CHUNK), BF16), jnp.zeros((CHUNK, CHUNK), BF16)
    for n in range(WIDTH // CHUNK):
        cols = slice(n * CHUNK, (n + 1) * CHUNK)
        order, part = win_ref[1:2, cols], win_ref[2:3, cols]
        picked = None
        for q in range(DEEP // CHUNK):
            rel = jnp.clip(order - CHUNK * q, -1, CHUNK).astype(F32).astype(BF16)
            onehot = jnp.where(iota == rel, one, zero)
            term = jnp.dot(
                rows[:, q * CHUNK : (q + 1) * CHUNK], onehot, preferred_element_type=F32
            )
            picked = term if picked is None else picked + term
        weights = leg_ref[:, cols].astype(F32)
        for t in range(2):
            cosine = picked[t * LATPAD : t * LATPAD + LAT]
            sine = picked[(2 + t) * LATPAD : (2 + t) * LATPAD + LAT]
            chosen = jnp.where(part > 0, sine, cosine)
            out_ref[0, t : t + 1, cols] = jnp.sum(chosen * weights, axis=0, keepdims=True)


def partial_coeffs(fields, legendre, window):
    kcoef = legendre.shape[1]
    return pl.pallas_call(
        spectral_kernel,
        grid=(kcoef // WIDTH,),
        in_specs=[
            pl.BlockSpec((2, LAT, NLON), lambda k: (0, 0, 0)),
            pl.BlockSpec((2, HALF, DEEP), lambda k: (0, 0, 0)),
            pl.BlockSpec((LAT, WIDTH), lambda k: (0, k)),
            pl.BlockSpec((3, WIDTH), lambda k: (0, k)),
        ],
        out_specs=pl.BlockSpec((1, 2, WIDTH), lambda k: (k, 0, 0)),
        out_shape=jax.ShapeDtypeStruct((kcoef // WIDTH, 2, WIDTH), F32),
        scratch_shapes=[pltpu.VMEM((4 * LATPAD, DEEP), BF16)],
        name="spectral",
    )(fields, jnp.asarray(half_basis()), legendre, window)


def exchange_kernel(
    part_ref, all_ref, row_ref, got, got1, own, far, send, rs, rs1, fs, ns, cs, ws, send2, keep
):
    i, j = lax.axis_index("tm"), lax.axis_index("lat")
    core, z, yh = i % 2, (i // 2) % 16, i // 32

    def tm_of(y_part, z_part, core_part):
        return (y_part * 16 + (z_part + 16) % 16) * 2 + core_part

    lats = [(j + d) % 8 for d in range(1, 8)]
    fars = []
    for y in range(2):
        for k in range(4):
            if y or k:
                fars.append(tm_of((yh + y) % 2, z + 4 * k, core))
    nears = [tm_of(yh, z + d, core) for d in (1, -1, 2, -2)]
    other = tm_of(yh, z, 1 - core)

    barrier = pltpu.get_barrier_semaphore()
    for peer in lats:
        pl.semaphore_signal(
            barrier, inc=1, device_id={"lat": peer}, device_id_type=pl.DeviceIdType.MESH
        )
    for peer in fars + nears + [other]:
        pl.semaphore_signal(
            barrier, inc=1, device_id={"tm": peer}, device_id_type=pl.DeviceIdType.MESH
        )
    pl.semaphore_wait(barrier, 7 + 7 + 4 + 1)

    def to(src, dst, send_sem, recv_sem, **peer):
        return pltpu.make_async_remote_copy(
            src_ref=src,
            dst_ref=dst,
            send_sem=send_sem,
            recv_sem=recv_sem,
            device_id=peer,
            device_id_type=pl.DeviceIdType.MESH,
        )

    copies = []
    for d, peer in enumerate(lats):
        copies.append(
            to(part_ref.at[0, :, pl.ds(0, PANEL)], got1.at[j], send.at[d], rs1.at[d], lat=peer)
        )
        copies.append(to(part_ref.at[peer], got.at[j], send.at[7 + d], rs.at[d], lat=peer))
    for copy in copies:
        copy.start()
    got[j] = part_ref[j]
    got1[j] = part_ref[0, :, :PANEL]
    for copy in copies:
        copy.wait()
    scale = F32(1.0 / math.sqrt(NLON))
    total, total1 = got[0], got1[0]
    for s in range(1, 8):
        total, total1 = total + got[s], total1 + got1[s]
    own[:, :WIDTH] = (total * scale).astype(BF16)
    own[:, WIDTH:] = (total1 * scale).astype(BF16)

    mine = (z // 4) * 2 + yh
    copies = [
        to(own, far.at[mine], send.at[d], fs.at[d], tm=peer) for d, peer in enumerate(fars)
    ]
    for copy in copies:
        copy.start()
    far[mine] = own[...]
    for copy in copies:
        copy.wait()
    pieces = [far[s].astype(F32) for s in range(8)]
    all_ref[0] = jnp.concatenate(pieces, axis=0).astype(BF16)

    top, bottom = pl.ds(0, 8), pl.ds(8, 8)
    near = [
        to(all_ref.at[0], all_ref.at[2], send.at[0], ns.at[0], tm=nears[0]),
        to(all_ref.at[0], all_ref.at[1], send.at[1], ns.at[1], tm=nears[1]),
        to(all_ref.at[0, top], all_ref.at[3, top], send.at[2], ns.at[2], tm=nears[2]),
        to(all_ref.at[0, bottom], all_ref.at[3, bottom], send.at[3], ns.at[3], tm=nears[3]),
    ]
    across = [
        to(all_ref.at[s], all_ref.at[4 + s], send2.at[s], cs.at[s], tm=other) for s in range(4)
    ]
    for copy in near:
        copy.start()
    across[0].start()
    near[0].wait_recv()
    across[2].start()
    near[1].wait_recv()
    across[1].start()
    near[2].wait_recv()
    near[3].wait_recv()
    across[3].start()
    for copy in across:
        copy.wait_recv()
    for copy in near + across:
        copy.wait_send()

    root = i // 8
    lanes = pl.ds(pl.multiple_of((i % 8) * BLOCK, BLOCK), BLOCK)

    @pl.when(j == root)
    def _():
        out = [
            to(all_ref.at[:, :, lanes], row_ref, send.at[d], ws, lat=peer)
            for d, peer in enumerate(lats)
        ]
        for copy in out:
            copy.start()
        here = pltpu.make_async_copy(all_ref.at[:, :, lanes], row_ref, keep)
        here.start()
        here.wait()
        for copy in out:
            copy.wait_send()

    @pl.when(j != root)
    def _():
        to(all_ref.at[:, :, lanes], row_ref, send.at[0], ws, lat=root).wait_recv()


def exchange(parts):
    dma = pltpu.SemaphoreType.DMA
    return pl.pallas_call(
        exchange_kernel,
        in_specs=[pl.BlockSpec(memory_space=pltpu.VMEM)],
        out_specs=[pl.BlockSpec(memory_space=pltpu.VMEM)] * 2,
        out_shape=[
            jax.ShapeDtypeStruct((8, 16, SENT), BF16),
            jax.ShapeDtypeStruct((8, 16, BLOCK), BF16),
        ],
        scratch_shapes=[
            pltpu.VMEM((8, 2, WIDTH), F32),
            pltpu.VMEM((8, 2, PANEL), F32),
            pltpu.VMEM((2, SENT), BF16),
            pltpu.VMEM((8, 2, SENT), BF16),
            dma((14,)),
            dma((7,)),
            dma((7,)),
            dma((7,)),
            dma((4,)),
            dma((4,)),
            dma(()),
            dma((4,)),
            dma(()),
        ],
        compiler_params=pltpu.CompilerParams(collective_id=0, has_side_effects=True),
        name="exchange",
    )(parts)


def split(x):
    high = x.astype(BF16)
    return high, (x - high.astype(F32)).astype(BF16)


def contract(left, right, dims):
    def dot(a, b):
        return lax.dot_general(a, b, (dims, ((), ())), preferred_element_type=F32)

    lefts = (left,) if left.dtype == BF16 else split(left)
    rights = (right,) if right.dtype == BF16 else split(right)
    total = dot(lefts[0], rights[0])
    if len(lefts) > 1:
        total = total + dot(lefts[1], rights[0])
    if len(rights) > 1:
        total = total + dot(lefts[0], rights[1])
    return total


ROWS = ((0,), (0,))
LANES = ((1,), (1,))
PLAIN = ((1,), (0,))


def eliminate(spd, rhs, upper_ref, solved_ref, panel=32, group=8):
    count, size = len(spd), BLOCK
    for b in range(count):
        upper_ref[b] = spd[b]
        solved_ref[b] = rhs[b]
    sub = lax.broadcasted_iota(jnp.int32, (panel, size), 0)
    for p in range(0, size, panel):
        x = [upper_ref[b, p : p + panel, :] for b in range(count)]
        y = [solved_ref[b, p : p + panel, :] for b in range(count)]
        scale = [jnp.ones((panel, size), F32) for _ in range(count)]
        for start in range(0, panel, group):
            column = [
                [
                    jnp.broadcast_to(x[b][:, p + start + m : p + start + m + 1], (panel, size))
                    for m in range(group)
                ]
                for b in range(count)
            ]
            for m in range(group):
                k = start + m
                for b in range(count):
                    c = column[b][m]
                    pivot = jnp.broadcast_to(c[k : k + 1, :], (panel, size))
                    factor = jnp.where(sub > k, c * (1.0 / pivot), 0.0)
                    scale[b] = jnp.where(sub == k, lax.rsqrt(pivot), scale[b])
                    for later in range(m + 1, group):
                        u = column[b][later]
                        column[b][later] = u - factor * u[k : k + 1, :]
                    x[b] = x[b] - factor * x[b][k : k + 1, :]
                    y[b] = y[b] - factor * y[b][k : k + 1, :]
        for b in range(count):
            x[b], y[b] = x[b] * scale[b], y[b] * scale[b]
            upper_ref[b, p : p + panel, :] = x[b]
            solved_ref[b, p : p + panel, :] = y[b]
            if p + panel < size:
                below = x[b][:, p + panel :]
                upper_ref[b, p + panel :, :] -= contract(below, x[b], ROWS)
                solved_ref[b, p + panel :, :] -= contract(below, y[b], ROWS)


def panel_kernel(all_ref, row_ref, win_ref, ridge_ref, out_ref, upper, solved, upper2, solved2):
    i, j = lax.axis_index("tm"), lax.axis_index("lat")
    ridge = ridge_ref[0]

    def lam_of(degree):
        return ridge * (1.0 + (degree * (degree + 1)).astype(F32) / float(LMAX * (LMAX + 1)))

    lam = lam_of(win_ref[0:1, :PANEL])
    row_id = lax.broadcasted_iota(jnp.int32, (BLOCK, BLOCK), 0)
    col_id = lax.broadcasted_iota(jnp.int32, (BLOCK, BLOCK), 1)
    eye = (row_id == col_id).astype(F32)
    inverse = F32(1.0 / NT)
    blocks = [
        all_ref[:, :, WIDTH + BLOCK * b : WIDTH + BLOCK * (b + 1)].reshape(NT, BLOCK)
        for b in range(4)
    ]
    cols = all_ref[:, :, :WIDTH].reshape(NT, WIDTH)
    rows = row_ref[...].reshape(NT, BLOCK)
    lams = [lam[:, BLOCK * b : BLOCK * (b + 1)] for b in range(4)]

    total, spd = eye, []
    for b in range(4):
        total = total + contract(blocks[b].astype(F32) * (inverse / lams[b]), blocks[b], LANES)
        spd.append(total)
    eliminate(spd, [eye] * 4, upper, solved)
    spd, rhs = [], []
    for b in range(4):
        if b == 0:
            spd.append(contract(blocks[0], blocks[0], ROWS) * inverse + eye * lams[0])
            rhs.append(blocks[0].astype(F32).T)
        else:
            low = solved[b - 1]
            first = contract(low, blocks[b], PLAIN)
            spd.append(contract(first, first, ROWS) * inverse + eye * lams[b])
            rhs.append(contract(first, low, ROWS))
    eliminate(spd, rhs, upper2, solved2)

    @pl.when(i < 4)
    def _():
        out_ref[...] = contract(solved2[i], cols, PLAIN) * inverse

    @pl.when(i >= 4)
    def _():
        low = solved[3]
        first = contract(low, rows, PLAIN)
        left = contract(first, low, ROWS)
        start = pl.multiple_of(j * WIDTH, WIDTH)
        lam_cols = lam_of(win_ref[0:1, pl.ds(start, WIDTH)])
        row_glob = i * BLOCK + lax.broadcasted_iota(jnp.int32, (BLOCK, WIDTH), 0)
        col_glob = j * WIDTH + lax.broadcasted_iota(jnp.int32, (BLOCK, WIDTH), 1)
        out_ref[...] = contract(left, cols, PLAIN) * inverse + jnp.where(
            row_glob == col_glob, lam_cols, 0.0
        )

    @pl.when(j == 0)
    def _():
        for b in range(4):
            lower = jnp.where(row_id >= col_id, upper2[b].T, 0.0)
            below = contract(rows, solved2[b], ((0,), (1,))) * inverse
            out_ref[:, BLOCK * b : BLOCK * (b + 1)] = jnp.where(
                i > b, below, jnp.where(i == b, lower, 0.0)
            )


def panel_step(everyone, rows, window, ridge):
    vmem = pl.BlockSpec(memory_space=pltpu.VMEM)
    return pl.pallas_call(
        panel_kernel,
        in_specs=[vmem, vmem, vmem, pl.BlockSpec(memory_space=pltpu.SMEM)],
        out_specs=vmem,
        out_shape=jax.ShapeDtypeStruct((BLOCK, WIDTH), F32),
        scratch_shapes=[pltpu.VMEM((4, BLOCK, BLOCK), F32)] * 4,
        name="panel",
    )(everyone, rows, window, ridge)


def on_device(fields, legendre, order_table, window_start, ridge):
    window = lax.dynamic_slice_in_dim(order_table, window_start[0], legendre.shape[1], 1)
    parts = partial_coeffs(fields, legendre, window)
    everyone, rows = exchange(parts)
    return panel_step(everyone, rows, window, ridge)


def solution(mesh):
    placed = (P("tm", "lat", None), P("lat", None), P(), P(), P())
    return jax.shard_map(
        on_device, mesh=mesh, in_specs=placed, out_specs=P("tm", "lat"), check_vma=False
    )
```

```python
import math

import jax
import jax.numpy as jnp
import numpy as np
from jax import lax
from jax.experimental import pallas as pl
from jax.experimental.pallas import tpu as pltpu
from jax.sharding import PartitionSpec as P

NLON = 1440
HALF = NLON // 2
LMAX = 720
NT = 128
PANEL = 512
BLOCK = 128
WIDTH = 1024
SENT = WIDTH + PANEL
LAT = 90
LATPAD = 96
DEEP = 768
CHUNK = 256
F32 = jnp.float32
BF16 = jnp.bfloat16


def half_basis():
    n = np.arange(HALF)[:, None]
    c = np.arange(HALF)[None, :]
    phase = ((n * c) % NLON).astype(np.float32) * np.float32(2.0 * math.pi / NLON)
    basis = np.zeros((2, HALF, DEEP), np.float32)
    basis[0, :, :HALF] = np.cos(phase)
    basis[1, :, :HALF] = np.sin(phase)
    return basis.astype(BF16)


FARS = (6, 0, 3, -3, -6)
NEARS = ((0, 0, 5), (1, 5, 5), (-1, 10, 5), (2, 15, 1))


def coeff_kernel(
    fields_hbm,
    basis_hbm,
    leg_hbm,
    table_hbm,
    all_ref,
    row_ref,
    fields,
    basis,
    leg,
    table,
    spectra,
    rows,
    part,
    got,
    got1,
    load,
    legs,
    lat_send,
    lat_recv,
    far_send,
    far_recv,
    near_send,
    near_recv,
    core_send,
    core_recv,
    row_send,
    row_recv,
    keep,
):
    i, j = lax.axis_index("tm"), lax.axis_index("lat")
    core, z, yh = i % 2, (i // 2) % 16, i // 32
    mesh_ids = pl.DeviceIdType.MESH

    def tm_of(y_part, z_part, core_part):
        return (y_part * 16 + (z_part + 16) % 16) * 2 + core_part

    lats = [(j + d) % 8 for d in range(1, 8)]
    other = tm_of(yh, z, 1 - core)
    greeted = [tm_of(yh, z + d, core) for d in (3, -3, 6, -6, 1, -1, 2, -2)]
    greeted += [tm_of(1 - yh, z + d, core) for d in (0, 1, -1, 2, -2)]
    greeted += [other]

    loads = [
        pltpu.make_async_copy(fields_hbm, fields, load.at[0]),
        pltpu.make_async_copy(basis_hbm.at[0], basis.at[0], load.at[1]),
        pltpu.make_async_copy(basis_hbm.at[1], basis.at[1], load.at[2]),
        pltpu.make_async_copy(table_hbm, table, load.at[3]),
    ]
    for copy in loads:
        copy.start()

    def leg_copy(k):
        cols = pl.ds(pl.multiple_of(k * WIDTH, WIDTH), WIDTH)
        return pltpu.make_async_copy(leg_hbm.at[:, cols], leg.at[k], legs.at[k])

    for k in range(8):
        leg_copy(k).start()
    barrier = pltpu.get_barrier_semaphore()
    for peer in lats:
        pl.semaphore_signal(barrier, inc=1, device_id={"lat": peer}, device_id_type=mesh_ids)
    for peer in greeted:
        pl.semaphore_signal(barrier, inc=1, device_id={"tm": peer}, device_id_type=mesh_ids)

    loads[0].wait()
    lane = lax.broadcasted_iota(jnp.int32, (1, DEEP), 1)
    sign = jnp.where(lane % 2 == 0, 1.0, -1.0).astype(F32)
    flat = fields[...].reshape(2 * LAT, NLON)
    low, high = flat[:, :HALF], flat[:, HALF:]
    for p in range(2):
        loads[1 + p].wait()
        first = jnp.dot(low, basis[p], preferred_element_type=F32)
        second = jnp.dot(high, basis[p], preferred_element_type=F32)
        both = first + sign * second
        for v in range(DEEP // 128):
            lanes = slice(v * 128, (v + 1) * 128)
            spectra[v] = both[:, lanes]
            for t in range(2):
                at = (2 * p + t) * LATPAD
                rows[at : at + LAT, lanes] = spectra[v, pl.ds(t, LAT, stride=2), :].astype(BF16)

    loads[3].wait()
    iota = lax.broadcasted_iota(jnp.int32, (CHUNK, CHUNK), 0).astype(F32).astype(BF16)
    one, zero = jnp.ones((CHUNK, CHUNK), BF16), jnp.zeros((CHUNK, CHUNK), BF16)

    def tile(k, carry):
        leg_copy(k).wait()
        window = table[:, pl.ds(pl.multiple_of(k * WIDTH, WIDTH), WIDTH)]
        for n in range(WIDTH // CHUNK):
            cols = slice(n * CHUNK, (n + 1) * CHUNK)
            order, sine_part = window[1:2, cols], window[2:3, cols]
            picked = None
            for q in range(DEEP // CHUNK):
                rel = jnp.clip(order - CHUNK * q, -1, CHUNK).astype(F32).astype(BF16)
                onehot = jnp.where(iota == rel, one, zero)
                term = jnp.dot(
                    rows[:, q * CHUNK : (q + 1) * CHUNK], onehot, preferred_element_type=F32
                )
                picked = term if picked is None else picked + term
            weights = leg[k, :, cols].astype(F32)
            for t in range(2):
                cosine = picked[t * LATPAD : t * LATPAD + LAT]
                sine = picked[(2 + t) * LATPAD : (2 + t) * LATPAD + LAT]
                chosen = jnp.where(sine_part > 0, sine, cosine)
                part[k, t : t + 1, cols] = jnp.sum(chosen * weights, axis=0, keepdims=True)
        return carry

    lax.fori_loop(0, 8, tile, 0)

    pl.semaphore_wait(barrier, 7 + 14)

    def to(src, dst, send_sem, recv_sem, **peer):
        return pltpu.make_async_remote_copy(
            src_ref=src,
            dst_ref=dst,
            send_sem=send_sem,
            recv_sem=recv_sem,
            device_id=peer,
            device_id_type=mesh_ids,
        )

    copies = []
    for d, peer in enumerate(lats):
        sems = (lat_send.at[2 * d], lat_recv.at[2 * d])
        copies.append(to(part.at[0, :, pl.ds(0, PANEL)], got1.at[j], *sems, lat=peer))
        sems = (lat_send.at[2 * d + 1], lat_recv.at[2 * d + 1])
        copies.append(to(part.at[peer], got.at[j], *sems, lat=peer))
    for copy in copies:
        copy.start()
    got[j] = part[j]
    got1[j] = part[0, :, :PANEL]
    for copy in copies:
        copy.wait_recv()
    scale = F32(1.0 / math.sqrt(NLON))
    total, total1 = got[0], got1[0]
    for s in range(1, 8):
        total, total1 = total + got[s], total1 + got1[s]
    all_ref[1, :, :WIDTH] = (total * scale).astype(BF16)
    all_ref[1, :, WIDTH:] = (total1 * scale).astype(BF16)

    far = []
    for s, a in enumerate(FARS):
        if a:
            far.append(
                to(
                    all_ref.at[1],
                    all_ref.at[s],
                    far_send.at[s],
                    far_recv.at[s],
                    tm=tm_of(yh, z - a, core),
                )
            )
    for copy in far:
        copy.start()
    for copy in far:
        copy.wait_recv()

    near, across = [], []
    for y in range(2):
        for b, at, count in NEARS:
            k = len(across)
            here = pl.ds(16 * y + at, count)
            if y or b:
                near.append(
                    to(
                        all_ref.at[pl.ds(0, count)],
                        all_ref.at[here],
                        near_send.at[k],
                        near_recv.at[k],
                        tm=tm_of(yh if y == 0 else 1 - yh, z - b, core),
                    )
                )
            else:
                near.append(None)
            across.append(
                to(
                    all_ref.at[here],
                    all_ref.at[pl.ds(32 + 16 * y + at, count)],
                    core_send.at[k],
                    core_recv.at[k],
                    tm=other,
                )
            )
    for copy in near:
        if copy is not None:
            copy.start()
    for copy, onward in zip(near, across):
        if copy is not None:
            copy.wait_recv()
        onward.start()
    for copy in across:
        copy.wait_recv()

    root = i // 8
    lanes = pl.ds(pl.multiple_of((i % 8) * BLOCK, BLOCK), BLOCK)

    @pl.when(j == root)
    def _():
        out = [
            to(all_ref.at[:, :, lanes], row_ref, row_send.at[d], row_recv, lat=peer)
            for d, peer in enumerate(lats)
        ]
        for copy in out:
            copy.start()
        here = pltpu.make_async_copy(all_ref.at[:, :, lanes], row_ref, keep)
        here.start()
        here.wait()
        for copy in out:
            copy.wait_send()

    @pl.when(j != root)
    def _():
        to(all_ref.at[:, :, lanes], row_ref, row_send.at[0], row_recv, lat=root).wait_recv()

    for copy in copies + far + [copy for copy in near if copy is not None] + across:
        copy.wait_send()


def coefficients(fields, legendre, window):
    dma = pltpu.SemaphoreType.DMA
    hbm = pl.BlockSpec(memory_space=pl.ANY)
    vmem = pl.BlockSpec(memory_space=pltpu.VMEM)
    return pl.pallas_call(
        coeff_kernel,
        in_specs=[hbm] * 4,
        out_specs=[vmem, vmem],
        out_shape=[
            jax.ShapeDtypeStruct((64, 2, SENT), BF16),
            jax.ShapeDtypeStruct((64, 2, BLOCK), BF16),
        ],
        scratch_shapes=[
            pltpu.VMEM((LAT, 2, NLON), BF16),
            pltpu.VMEM((2, HALF, DEEP), BF16),
            pltpu.VMEM((8, LAT, WIDTH), BF16),
            pltpu.VMEM((3, 8 * WIDTH), jnp.int32),
            pltpu.VMEM((DEEP // 128, 2 * LAT, 128), F32),
            pltpu.VMEM((4 * LATPAD, DEEP), BF16),
            pltpu.VMEM((8, 2, WIDTH), F32),
            pltpu.VMEM((8, 2, WIDTH), F32),
            pltpu.VMEM((8, 2, PANEL), F32),
            dma((4,)),
            dma((8,)),
            dma((14,)),
            dma((14,)),
            dma((5,)),
            dma((5,)),
            dma((8,)),
            dma((8,)),
            dma((8,)),
            dma((8,)),
            dma((7,)),
            dma(()),
            dma(()),
        ],
        compiler_params=pltpu.CompilerParams(collective_id=0, has_side_effects=True),
        name="coeffs",
    )(
        jnp.transpose(fields, (1, 0, 2)),
        jnp.asarray(half_basis()),
        legendre,
        window,
    )


def split(x):
    high = x.astype(BF16)
    return high, (x - high.astype(F32)).astype(BF16)


def contract(left, right, dims):
    def dot(a, b):
        return lax.dot_general(a, b, (dims, ((), ())), preferred_element_type=F32)

    lefts = (left,) if left.dtype == BF16 else split(left)
    rights = (right,) if right.dtype == BF16 else split(right)
    total = dot(lefts[0], rights[0])
    if len(lefts) > 1:
        total = total + dot(lefts[1], rights[0])
    if len(rights) > 1:
        total = total + dot(lefts[0], rights[1])
    return total


ROWS = ((0,), (0,))
LANES = ((1,), (1,))
PLAIN = ((1,), (0,))


def eliminate(spd, rhs, upper_ref, solved_ref, panel=32, group=8):
    count, size = len(spd), BLOCK
    for b in range(count):
        upper_ref[b] = spd[b]
        solved_ref[b] = rhs[b]
    sub = lax.broadcasted_iota(jnp.int32, (panel, size), 0)
    for p in range(0, size, panel):
        x = [upper_ref[b, p : p + panel, :] for b in range(count)]
        y = [solved_ref[b, p : p + panel, :] for b in range(count)]
        scale = [jnp.ones((panel, size), F32) for _ in range(count)]
        for start in range(0, panel, group):
            column = [
                [
                    jnp.broadcast_to(x[b][:, p + start + m : p + start + m + 1], (panel, size))
                    for m in range(group)
                ]
                for b in range(count)
            ]
            for m in range(group):
                k = start + m
                for b in range(count):
                    c = column[b][m]
                    pivot = jnp.broadcast_to(c[k : k + 1, :], (panel, size))
                    factor = jnp.where(sub > k, c * (1.0 / pivot), 0.0)
                    scale[b] = jnp.where(sub == k, lax.rsqrt(pivot), scale[b])
                    for later in range(m + 1, group):
                        u = column[b][later]
                        column[b][later] = u - factor * u[k : k + 1, :]
                    x[b] = x[b] - factor * x[b][k : k + 1, :]
                    y[b] = y[b] - factor * y[b][k : k + 1, :]
        for b in range(count):
            x[b], y[b] = x[b] * scale[b], y[b] * scale[b]
            upper_ref[b, p : p + panel, :] = x[b]
            solved_ref[b, p : p + panel, :] = y[b]
            if p + panel < size:
                below = x[b][:, p + panel :]
                upper_ref[b, p + panel :, :] -= contract(below, x[b], ROWS)
                solved_ref[b, p + panel :, :] -= contract(below, y[b], ROWS)


def panel_kernel(all_ref, row_ref, win_ref, ridge_ref, out_ref, upper, solved, upper2, solved2):
    i, j = lax.axis_index("tm"), lax.axis_index("lat")
    ridge = ridge_ref[0]

    def lam_of(degree):
        return ridge * (1.0 + (degree * (degree + 1)).astype(F32) / float(LMAX * (LMAX + 1)))

    lam = lam_of(win_ref[0:1, :PANEL])
    row_id = lax.broadcasted_iota(jnp.int32, (BLOCK, BLOCK), 0)
    col_id = lax.broadcasted_iota(jnp.int32, (BLOCK, BLOCK), 1)
    eye = (row_id == col_id).astype(F32)
    inverse = F32(1.0 / NT)
    whole = all_ref[...].reshape(NT, SENT)
    cols = whole[:, :WIDTH]
    blocks = [whole[:, WIDTH + BLOCK * b : WIDTH + BLOCK * (b + 1)] for b in range(4)]
    rows = row_ref[...].reshape(NT, BLOCK)
    lams = [lam[:, BLOCK * b : BLOCK * (b + 1)] for b in range(4)]

    total, spd = eye, []
    for b in range(4):
        total = total + contract(blocks[b].astype(F32) * (inverse / lams[b]), blocks[b], LANES)
        spd.append(total)
    eliminate(spd, [eye] * 4, upper, solved)
    spd, rhs = [], []
    for b in range(4):
        if b == 0:
            spd.append(contract(blocks[0], blocks[0], ROWS) * inverse + eye * lams[0])
            rhs.append(blocks[0].astype(F32).T)
        else:
            low = solved[b - 1]
            first = contract(low, blocks[b], PLAIN)
            spd.append(contract(first, first, ROWS) * inverse + eye * lams[b])
            rhs.append(contract(first, low, ROWS))
    eliminate(spd, rhs, upper2, solved2)

    @pl.when(i < 4)
    def _():
        out_ref[...] = contract(solved2[i], cols, PLAIN) * inverse

    @pl.when(i >= 4)
    def _():
        low = solved[3]
        first = contract(low, rows, PLAIN)
        left = contract(first, low, ROWS)
        start = pl.multiple_of(j * WIDTH, WIDTH)
        lam_cols = lam_of(win_ref[0:1, pl.ds(start, WIDTH)])
        row_glob = i * BLOCK + lax.broadcasted_iota(jnp.int32, (BLOCK, WIDTH), 0)
        col_glob = j * WIDTH + lax.broadcasted_iota(jnp.int32, (BLOCK, WIDTH), 1)
        out_ref[...] = contract(left, cols, PLAIN) * inverse + jnp.where(
            row_glob == col_glob, lam_cols, 0.0
        )

    @pl.when(j == 0)
    def _():
        for b in range(4):
            lower = jnp.where(row_id >= col_id, upper2[b].T, 0.0)
            below = contract(rows, solved2[b], ((0,), (1,))) * inverse
            out_ref[:, BLOCK * b : BLOCK * (b + 1)] = jnp.where(
                i > b, below, jnp.where(i == b, lower, 0.0)
            )


def panel_step(everyone, rows, window, ridge):
    vmem = pl.BlockSpec(memory_space=pltpu.VMEM)
    return pl.pallas_call(
        panel_kernel,
        in_specs=[vmem, vmem, vmem, pl.BlockSpec(memory_space=pltpu.SMEM)],
        out_specs=vmem,
        out_shape=jax.ShapeDtypeStruct((BLOCK, WIDTH), F32),
        scratch_shapes=[pltpu.VMEM((4, BLOCK, BLOCK), F32)] * 4,
        name="panel",
    )(everyone, rows, window, ridge)


def on_device(fields, legendre, order_table, window_start, ridge):
    window = lax.dynamic_slice_in_dim(order_table, window_start[0], legendre.shape[1], 1)
    everyone, rows = coefficients(fields, legendre, window)
    return panel_step(everyone, rows, window, ridge)


def solution(mesh):
    placed = (P("tm", "lat", None), P("lat", None), P(), P(), P())
    return jax.shard_map(
        on_device, mesh=mesh, in_specs=placed, out_specs=P("tm", "lat"), check_vma=False
    )
```

```python
import math

import jax
import jax.numpy as jnp
import numpy as np
from jax import lax
from jax.experimental import pallas as pl
from jax.experimental.pallas import tpu as pltpu
from jax.sharding import PartitionSpec as P

NLON = 1440
HALF = NLON // 2
LMAX = 720
NT = 128
PANEL = 512
BLOCK = 128
WIDTH = 1024
LAT = 90
LATPAD = 96
DEEP = 768
CHUNK = 256
F32 = jnp.float32
BF16 = jnp.bfloat16


def half_basis():
    n = np.arange(HALF)[:, None]
    c = np.arange(HALF)[None, :]
    phase = ((n * c) % NLON).astype(np.float32) * np.float32(2.0 * math.pi / NLON)
    basis = np.zeros((2, HALF, DEEP), np.float32)
    basis[0, :, :HALF] = np.cos(phase)
    basis[1, :, :HALF] = np.sin(phase)
    return basis.astype(BF16)


def split(x):
    high = x.astype(BF16)
    return high, (x - high.astype(F32)).astype(BF16)


def contract(left, right, dims):
    def dot(a, b):
        return lax.dot_general(a, b, (dims, ((), ())), preferred_element_type=F32)

    lefts = (left,) if left.dtype == BF16 else split(left)
    rights = (right,) if right.dtype == BF16 else split(right)
    total = dot(lefts[0], rights[0])
    if len(lefts) > 1:
        total = total + dot(lefts[1], rights[0])
    if len(rights) > 1:
        total = total + dot(lefts[0], rights[1])
    return total


ROWS = ((0,), (0,))
LANES = ((1,), (1,))
PLAIN = ((1,), (0,))


def eliminate(spd, rhs, upper_ref, solved_ref, between=(), panel=32):
    count, size = len(spd), BLOCK
    for b in range(count):
        upper_ref[b] = spd[b]
        solved_ref[b] = rhs[b]
    sub = lax.broadcasted_iota(jnp.int32, (8, size), 0)
    pieces = panel // 8
    for p in range(0, size, panel):
        at = [slice(p + 8 * r, p + 8 * r + 8) for r in range(pieces)]
        x = [[upper_ref[b, rows, :] for rows in at] for b in range(count)]
        y = [[solved_ref[b, rows, :] for rows in at] for b in range(count)]
        for g in range(pieces):
            lane = p + 8 * g
            column = [
                [
                    [
                        jnp.broadcast_to(x[b][r][:, lane + m : lane + m + 1], (8, size))
                        for r in range(g, pieces)
                    ]
                    for m in range(8)
                ]
                for b in range(count)
            ]
            scale = [jnp.ones((8, size), F32) for _ in range(count)]
            for m in range(8):
                for b in range(count):
                    c = column[b][m]
                    root = lax.rsqrt(jnp.broadcast_to(c[0][m : m + 1, :], (8, size)))
                    inverse = root * root
                    scale[b] = jnp.where(sub == m, root, scale[b])
                    x_row = jnp.broadcast_to(x[b][g][m : m + 1, :], (8, size))
                    y_row = jnp.broadcast_to(y[b][g][m : m + 1, :], (8, size))
                    u_rows = [
                        jnp.broadcast_to(column[b][later][0][m : m + 1, :], (8, size))
                        for later in range(m + 1, 8)
                    ]
                    for r in range(g, pieces):
                        factor = c[r - g] * inverse
                        if r == g:
                            factor = jnp.where(sub > m, factor, 0.0)
                        for later in range(m + 1, 8):
                            u = column[b][later]
                            u[r - g] = u[r - g] - factor * u_rows[later - m - 1]
                        x[b][r] = x[b][r] - factor * x_row
                        y[b][r] = y[b][r] - factor * y_row
            for b in range(count):
                x[b][g], y[b][g] = x[b][g] * scale[b], y[b][g] * scale[b]
                upper_ref[b, at[g], :] = x[b][g]
                solved_ref[b, at[g], :] = y[b][g]
        if p + panel < size:
            for b in range(count):
                xs, ys = jnp.concatenate(x[b], axis=0), jnp.concatenate(y[b], axis=0)
                below = xs[:, p + panel :]
                upper_ref[b, p + panel :, :] -= contract(below, xs, ROWS)
                solved_ref[b, p + panel :, :] -= contract(below, ys, ROWS)
        if p // panel < len(between):
            between[p // panel]()


FARS = (6, 0, 3, -3, -6)
NEARS = ((0, 0, 5), (1, 5, 5), (-1, 10, 5), (2, 15, 1))


def whole_kernel(
    fields_hbm,
    basis_hbm,
    leg_hbm,
    table_hbm,
    ridge_ref,
    out_ref,
    firsts,
    wides,
    row_ref,
    fields,
    basis,
    leg,
    table,
    spectra,
    rows,
    part,
    got,
    got1,
    load,
    legs,
    lat_send,
    lat_recv,
    far_send,
    far_recv,
    near_send,
    near_recv,
    core_send,
    core_recv,
    row_send,
    row_recv,
    keep,
    upper,
    solved,
    upper2,
    solved2,
):
    i, j = lax.axis_index("tm"), lax.axis_index("lat")
    core, z, yh = i % 2, (i // 2) % 16, i // 32
    mesh_ids = pl.DeviceIdType.MESH

    def tm_of(y_part, z_part, core_part):
        return (y_part * 16 + (z_part + 16) % 16) * 2 + core_part

    lats = [(j + d) % 8 for d in range(1, 8)]
    other = tm_of(yh, z, 1 - core)
    greeted = [tm_of(yh, z + d, core) for d in (3, -3, 6, -6, 1, -1, 2, -2)]
    greeted += [tm_of(1 - yh, z + d, core) for d in (0, 1, -1, 2, -2)]
    greeted += [other]

    loads = [
        pltpu.make_async_copy(fields_hbm, fields, load.at[0]),
        pltpu.make_async_copy(basis_hbm.at[0], basis.at[0], load.at[1]),
        pltpu.make_async_copy(basis_hbm.at[1], basis.at[1], load.at[2]),
        pltpu.make_async_copy(table_hbm, table, load.at[3]),
    ]
    for copy in loads:
        copy.start()

    def leg_copy(k):
        cols = pl.ds(pl.multiple_of(k * WIDTH, WIDTH), WIDTH)
        return pltpu.make_async_copy(leg_hbm.at[:, cols], leg.at[k], legs.at[k])

    for k in range(8):
        leg_copy(k).start()
    barrier = pltpu.get_barrier_semaphore()
    for peer in lats:
        pl.semaphore_signal(barrier, inc=1, device_id={"lat": peer}, device_id_type=mesh_ids)
    for peer in greeted:
        pl.semaphore_signal(barrier, inc=1, device_id={"tm": peer}, device_id_type=mesh_ids)

    loads[0].wait()
    lane = lax.broadcasted_iota(jnp.int32, (1, DEEP), 1)
    sign = jnp.where(lane % 2 == 0, 1.0, -1.0).astype(F32)
    flat = fields[...].reshape(2 * LAT, NLON)
    low, high = flat[:, :HALF], flat[:, HALF:]
    for p in range(2):
        loads[1 + p].wait()
        first = jnp.dot(low, basis[p], preferred_element_type=F32)
        second = jnp.dot(high, basis[p], preferred_element_type=F32)
        both = first + sign * second
        for v in range(DEEP // 128):
            lanes = slice(v * 128, (v + 1) * 128)
            spectra[v] = both[:, lanes]
            for t in range(2):
                at = (2 * p + t) * LATPAD
                rows[at : at + LAT, lanes] = spectra[v, pl.ds(t, LAT, stride=2), :].astype(BF16)

    loads[3].wait()
    iota = lax.broadcasted_iota(jnp.int32, (CHUNK, CHUNK), 0).astype(F32).astype(BF16)
    one, zero = jnp.ones((CHUNK, CHUNK), BF16), jnp.zeros((CHUNK, CHUNK), BF16)

    def tile(k, carry):
        leg_copy(k).wait()
        window = table[:, pl.ds(pl.multiple_of(k * WIDTH, WIDTH), WIDTH)]
        for n in range(WIDTH // CHUNK):
            cols = slice(n * CHUNK, (n + 1) * CHUNK)
            order, sine_part = window[1:2, cols], window[2:3, cols]
            picked = None
            for q in range(DEEP // CHUNK):
                rel = jnp.clip(order - CHUNK * q, -1, CHUNK).astype(F32).astype(BF16)
                onehot = jnp.where(iota == rel, one, zero)
                term = jnp.dot(
                    rows[:, q * CHUNK : (q + 1) * CHUNK], onehot, preferred_element_type=F32
                )
                picked = term if picked is None else picked + term
            weights = leg[k, :, cols].astype(F32)
            for t in range(2):
                cosine = picked[t * LATPAD : t * LATPAD + LAT]
                sine = picked[(2 + t) * LATPAD : (2 + t) * LATPAD + LAT]
                chosen = jnp.where(sine_part > 0, sine, cosine)
                part[k, t : t + 1, cols] = jnp.sum(chosen * weights, axis=0, keepdims=True)
        return carry

    lax.fori_loop(0, 8, tile, 0)

    pl.semaphore_wait(barrier, 7 + 14)

    def to(src, dst, send_sem, recv_sem, **peer):
        return pltpu.make_async_remote_copy(
            src_ref=src,
            dst_ref=dst,
            send_sem=send_sem,
            recv_sem=recv_sem,
            device_id=peer,
            device_id_type=mesh_ids,
        )

    sets = (firsts, wides)
    parts = ((got1, PANEL), (got, WIDTH))
    lat_copies = ([], [])
    for n, (landing, width) in enumerate(parts):
        for d, peer in enumerate(lats):
            src = part.at[0, :, pl.ds(0, PANEL)] if n == 0 else part.at[peer]
            k = 7 * n + d
            lat_copies[n].append(
                to(src, landing.at[j], lat_send.at[k], lat_recv.at[k], lat=peer)
            )
        for copy in lat_copies[n]:
            copy.start()
    got1[j] = part[0, :, :PANEL]
    got[j] = part[j]

    scale = F32(1.0 / math.sqrt(NLON))
    far = ([], [])
    for n, (landing, _) in enumerate(parts):
        for copy in lat_copies[n]:
            copy.wait_recv()
        total = landing[0]
        for s in range(1, 8):
            total = total + landing[s]
        sets[n][1] = (total * scale).astype(BF16)
        for s, a in enumerate(FARS):
            if a:
                far[n].append(
                    to(
                        sets[n].at[1],
                        sets[n].at[s],
                        far_send.at[5 * n + s],
                        far_recv.at[5 * n + s],
                        tm=tm_of(yh, z - a, core),
                    )
                )
        for copy in far[n]:
            copy.start()

    near, across = ([], []), ([], [])
    for n in range(2):
        for y in range(2):
            for b, at, count in NEARS:
                k = 8 * n + len(across[n])
                here = pl.ds(16 * y + at, count)
                if y or b:
                    near[n].append(
                        to(
                            sets[n].at[pl.ds(0, count)],
                            sets[n].at[here],
                            near_send.at[k],
                            near_recv.at[k],
                            tm=tm_of(yh if y == 0 else 1 - yh, z - b, core),
                        )
                    )
                else:
                    near[n].append(None)
                across[n].append(
                    to(
                        sets[n].at[here],
                        sets[n].at[pl.ds(32 + 16 * y + at, count)],
                        core_send.at[k],
                        core_recv.at[k],
                        tm=other,
                    )
                )
        for copy in far[n]:
            copy.wait_recv()
        for copy in near[n]:
            if copy is not None:
                copy.start()
        across[n][0].start()

    def pass_on(n):
        for copy, onward in zip(near[n][1:], across[n][1:]):
            copy.wait_recv()
            onward.start()

    pass_on(0)
    for copy in across[0]:
        copy.wait_recv()

    root = i // 8
    lanes = pl.ds(pl.multiple_of((i % 8) * BLOCK, BLOCK), BLOCK)
    row_copies = [
        to(wides.at[:, :, lanes], row_ref, row_send.at[d], row_recv, lat=peer)
        for d, peer in enumerate(lats)
    ]
    here = pltpu.make_async_copy(wides.at[:, :, lanes], row_ref, keep)

    def send_rows():
        for copy in across[1]:
            copy.wait_recv()

        @pl.when(j == root)
        def _():
            for copy in row_copies:
                copy.start()
            here.start()

    def wait_rows():
        @pl.when(j == root)
        def _():
            here.wait()
            for copy in row_copies:
                copy.wait_send()

        @pl.when(j != root)
        def _():
            to(wides.at[:, :, lanes], row_ref, row_send.at[0], row_recv, lat=root).wait_recv()

    ridge = ridge_ref[0]

    def lam_of(degree):
        return ridge * (1.0 + (degree * (degree + 1)).astype(F32) / float(LMAX * (LMAX + 1)))

    lam = lam_of(table[0:1, :PANEL])
    row_id = lax.broadcasted_iota(jnp.int32, (BLOCK, BLOCK), 0)
    col_id = lax.broadcasted_iota(jnp.int32, (BLOCK, BLOCK), 1)
    eye = (row_id == col_id).astype(F32)
    inverse = F32(1.0 / NT)
    first_cols = firsts[...].reshape(NT, PANEL)
    blocks = [first_cols[:, BLOCK * b : BLOCK * (b + 1)] for b in range(4)]
    lams = [lam[:, BLOCK * b : BLOCK * (b + 1)] for b in range(4)]

    total, spd = eye, []
    for b in range(4):
        total = total + contract(blocks[b].astype(F32) * (inverse / lams[b]), blocks[b], LANES)
        spd.append(total)
    eliminate(spd, [eye] * 4, upper, solved, (lambda: pass_on(1), lambda: None, send_rows))
    spd, rhs = [], []
    for b in range(4):
        if b == 0:
            spd.append(contract(blocks[0], blocks[0], ROWS) * inverse + eye * lams[0])
            rhs.append(blocks[0].astype(F32).T)
        else:
            low = solved[b - 1]
            first = contract(low, blocks[b], PLAIN)
            spd.append(contract(first, first, ROWS) * inverse + eye * lams[b])
            rhs.append(contract(first, low, ROWS))
    eliminate(spd, rhs, upper2, solved2)
    wait_rows()
    cols = wides[...].reshape(NT, WIDTH)
    rows_own = row_ref[...].reshape(NT, BLOCK)

    @pl.when(i < 4)
    def _():
        out_ref[...] = contract(solved2[jnp.minimum(i, 3)], cols, PLAIN) * inverse

    @pl.when(i >= 4)
    def _():
        low = solved[3]
        first = contract(low, rows_own, PLAIN)
        left = contract(first, low, ROWS)
        own_cols = pl.ds(pl.multiple_of(j * WIDTH, WIDTH), WIDTH)
        lam_cols = lam_of(table[0:1, own_cols])
        row_glob = i * BLOCK + lax.broadcasted_iota(jnp.int32, (BLOCK, WIDTH), 0)
        col_glob = j * WIDTH + lax.broadcasted_iota(jnp.int32, (BLOCK, WIDTH), 1)
        out_ref[...] = contract(left, cols, PLAIN) * inverse + jnp.where(
            row_glob == col_glob, lam_cols, 0.0
        )

    @pl.when(j == 0)
    def _():
        for b in range(4):
            lower = jnp.where(row_id >= col_id, upper2[b].T, 0.0)
            below = contract(rows_own, solved2[b], ((0,), (1,))) * inverse
            out_ref[:, BLOCK * b : BLOCK * (b + 1)] = jnp.where(
                i > b, below, jnp.where(i == b, lower, 0.0)
            )

    sent = lat_copies[0] + lat_copies[1] + far[0] + far[1] + across[0] + across[1]
    for copy in sent + near[0][1:] + near[1][1:]:
        copy.wait_send()


def factored_tile(fields, legendre, window, ridge):
    dma = pltpu.SemaphoreType.DMA
    hbm = pl.BlockSpec(memory_space=pl.ANY)
    vmem = pl.BlockSpec(memory_space=pltpu.VMEM)
    return pl.pallas_call(
        whole_kernel,
        in_specs=[hbm] * 4 + [pl.BlockSpec(memory_space=pltpu.SMEM)],
        out_specs=vmem,
        out_shape=jax.ShapeDtypeStruct((BLOCK, WIDTH), F32),
        scratch_shapes=[
            pltpu.VMEM((64, 2, PANEL), BF16),
            pltpu.VMEM((64, 2, WIDTH), BF16),
            pltpu.VMEM((64, 2, BLOCK), BF16),
            pltpu.VMEM((LAT, 2, NLON), BF16),
            pltpu.VMEM((2, HALF, DEEP), BF16),
            pltpu.VMEM((8, LAT, WIDTH), BF16),
            pltpu.VMEM((3, 8 * WIDTH), jnp.int32),
            pltpu.VMEM((DEEP // 128, 2 * LAT, 128), F32),
            pltpu.VMEM((4 * LATPAD, DEEP), BF16),
            pltpu.VMEM((8, 2, WIDTH), F32),
            pltpu.VMEM((8, 2, WIDTH), F32),
            pltpu.VMEM((8, 2, PANEL), F32),
            dma((4,)),
            dma((8,)),
            dma((14,)),
            dma((14,)),
            dma((10,)),
            dma((10,)),
            dma((16,)),
            dma((16,)),
            dma((16,)),
            dma((16,)),
            dma((7,)),
            dma(()),
            dma(()),
        ]
        + [pltpu.VMEM((4, BLOCK, BLOCK), F32)] * 4,
        compiler_params=pltpu.CompilerParams(collective_id=0, has_side_effects=True),
        name="factored",
    )(
        jnp.transpose(fields, (1, 0, 2)),
        jnp.asarray(half_basis()),
        legendre,
        window,
        ridge,
    )


def on_device(fields, legendre, order_table, window_start, ridge):
    window = lax.dynamic_slice_in_dim(order_table, window_start[0], legendre.shape[1], 1)
    return factored_tile(fields, legendre, window, ridge)


def solution(mesh):
    placed = (P("tm", "lat", None), P("lat", None), P(), P(), P())
    return jax.shard_map(
        on_device, mesh=mesh, in_specs=placed, out_specs=P("tm", "lat"), check_vma=False
    )
```

```python
import math

import jax
import jax.numpy as jnp
import numpy as np
from jax import lax
from jax.experimental import pallas as pl
from jax.experimental.pallas import tpu as pltpu
from jax.sharding import PartitionSpec as P

NLON = 1440
HALF = NLON // 2
LMAX = 720
NT = 128
PANEL = 512
BLOCK = 128
WIDTH = 1024
LAT = 90
LATPAD = 96
DEEP = 768
CHUNK = 256
F32 = jnp.float32
BF16 = jnp.bfloat16


def half_basis():
    n = np.arange(HALF)[:, None]
    c = np.arange(HALF)[None, :]
    phase = ((n * c) % NLON).astype(np.float32) * np.float32(2.0 * math.pi / NLON)
    basis = np.zeros((2, HALF, DEEP), np.float32)
    basis[0, :, :HALF] = np.cos(phase)
    basis[1, :, :HALF] = np.sin(phase)
    return basis.astype(BF16)


def split(x):
    high = x.astype(BF16)
    return high, (x - high.astype(F32)).astype(BF16)


def contract(left, right, dims):
    def dot(a, b):
        return lax.dot_general(a, b, (dims, ((), ())), preferred_element_type=F32)

    lefts = (left,) if left.dtype == BF16 else split(left)
    rights = (right,) if right.dtype == BF16 else split(right)
    total = dot(lefts[0], rights[0])
    if len(lefts) > 1:
        total = total + dot(lefts[1], rights[0])
    if len(rights) > 1:
        total = total + dot(lefts[0], rights[1])
    return total


ROWS = ((0,), (0,))
LANES = ((1,), (1,))
PLAIN = ((1,), (0,))


def eliminate(spd, rhs, upper_ref, solved_ref, between=(), panel=32):
    count, size = len(spd), BLOCK
    for b in range(count):
        upper_ref[b] = spd[b]
        solved_ref[b] = rhs[b]
    sub = lax.broadcasted_iota(jnp.int32, (8, size), 0)
    pieces = panel // 8
    for p in range(0, size, panel):
        at = [slice(p + 8 * r, p + 8 * r + 8) for r in range(pieces)]
        x = [[upper_ref[b, rows, :] for rows in at] for b in range(count)]
        y = [[solved_ref[b, rows, :] for rows in at] for b in range(count)]
        for g in range(pieces):
            lane = p + 8 * g
            column = [
                [
                    [
                        jnp.broadcast_to(x[b][r][:, lane + m : lane + m + 1], (8, size))
                        for r in range(g, pieces)
                    ]
                    for m in range(8)
                ]
                for b in range(count)
            ]
            scale = [jnp.ones((8, size), F32) for _ in range(count)]
            for m in range(8):
                for b in range(count):
                    c = column[b][m]
                    root = lax.rsqrt(jnp.broadcast_to(c[0][m : m + 1, :], (8, size)))
                    inverse = root * root
                    scale[b] = jnp.where(sub == m, root, scale[b])
                    x_row = jnp.broadcast_to(x[b][g][m : m + 1, :], (8, size))
                    y_row = jnp.broadcast_to(y[b][g][m : m + 1, :], (8, size))
                    u_rows = [
                        jnp.broadcast_to(column[b][later][0][m : m + 1, :], (8, size))
                        for later in range(m + 1, 8)
                    ]
                    for r in range(g, pieces):
                        factor = c[r - g] * inverse
                        if r == g:
                            factor = jnp.where(sub > m, factor, 0.0)
                        for later in range(m + 1, 8):
                            u = column[b][later]
                            u[r - g] = u[r - g] - factor * u_rows[later - m - 1]
                        x[b][r] = x[b][r] - factor * x_row
                        y[b][r] = y[b][r] - factor * y_row
            for b in range(count):
                x[b][g], y[b][g] = x[b][g] * scale[b], y[b][g] * scale[b]
                upper_ref[b, at[g], :] = x[b][g]
                solved_ref[b, at[g], :] = y[b][g]
        if p + panel < size:
            for b in range(count):
                xs, ys = jnp.concatenate(x[b], axis=0), jnp.concatenate(y[b], axis=0)
                below = xs[:, p + panel :]
                upper_ref[b, p + panel :, :] -= contract(below, xs, ROWS)
                solved_ref[b, p + panel :, :] -= contract(below, ys, ROWS)
        if p // panel < len(between):
            between[p // panel]()


FARS = (6, 0, 3, -3, -6)
NEARS = ((0, 0, 5), (1, 5, 5), (-1, 10, 5), (2, 15, 1))


def whole_kernel(
    fields_hbm,
    basis_hbm,
    leg_hbm,
    table_hbm,
    ridge_ref,
    out_ref,
    firsts,
    wides,
    row_ref,
    fields,
    basis,
    leg,
    table,
    spectra,
    rows,
    part,
    got,
    got1,
    load,
    legs,
    lat_send,
    lat_recv,
    far_send,
    far_recv,
    near_send,
    near_recv,
    core_send,
    core_recv,
    row_send,
    row_recv,
    keep,
    upper,
    solved,
    upper2,
    solved2,
):
    i, j = lax.axis_index("tm"), lax.axis_index("lat")
    core, z, yh = i % 2, (i // 2) % 16, i // 32
    mesh_ids = pl.DeviceIdType.MESH

    def tm_of(y_part, z_part, core_part):
        return (y_part * 16 + (z_part + 16) % 16) * 2 + core_part

    lats = [(j + d) % 8 for d in range(1, 8)]
    other = tm_of(yh, z, 1 - core)
    greeted = [tm_of(yh, z + d, core) for d in (3, -3, 6, -6, 1, -1, 2, -2)]
    greeted += [tm_of(1 - yh, z + d, core) for d in (0, 1, -1, 2, -2)]
    greeted += [other]

    loads = [
        pltpu.make_async_copy(fields_hbm, fields, load.at[0]),
        pltpu.make_async_copy(basis_hbm.at[0], basis.at[0], load.at[1]),
        pltpu.make_async_copy(basis_hbm.at[1], basis.at[1], load.at[2]),
        pltpu.make_async_copy(table_hbm, table, load.at[3]),
    ]
    for copy in loads:
        copy.start()

    def leg_copy(k):
        cols = pl.ds(pl.multiple_of(k * WIDTH, WIDTH), WIDTH)
        return pltpu.make_async_copy(leg_hbm.at[:, cols], leg.at[k], legs.at[k])

    for k in range(8):
        leg_copy(k).start()
    barrier = pltpu.get_barrier_semaphore()
    for peer in lats:
        pl.semaphore_signal(barrier, inc=1, device_id={"lat": peer}, device_id_type=mesh_ids)
    for peer in greeted:
        pl.semaphore_signal(barrier, inc=1, device_id={"tm": peer}, device_id_type=mesh_ids)

    loads[0].wait()
    lane = lax.broadcasted_iota(jnp.int32, (1, DEEP), 1)
    sign = jnp.where(lane % 2 == 0, 1.0, -1.0).astype(F32)
    flat = fields[...].reshape(2 * LAT, NLON)
    low, high = flat[:, :HALF], flat[:, HALF:]
    for p in range(2):
        loads[1 + p].wait()
        first = jnp.dot(low, basis[p], preferred_element_type=F32)
        second = jnp.dot(high, basis[p], preferred_element_type=F32)
        both = first + sign * second
        for v in range(DEEP // 128):
            lanes = slice(v * 128, (v + 1) * 128)
            spectra[v] = both[:, lanes]
            for t in range(2):
                at = (2 * p + t) * LATPAD
                rows[at : at + LAT, lanes] = spectra[v, pl.ds(t, LAT, stride=2), :].astype(BF16)

    loads[3].wait()
    iota = lax.broadcasted_iota(jnp.int32, (CHUNK, CHUNK), 0).astype(F32).astype(BF16)
    one, zero = jnp.ones((CHUNK, CHUNK), BF16), jnp.zeros((CHUNK, CHUNK), BF16)

    def pick(k, window, n):
        cols = slice(n * CHUNK, (n + 1) * CHUNK)
        order, sine_part = window[1:2, cols], window[2:3, cols]
        picked = None
        for q in range(DEEP // CHUNK):
            rel = jnp.clip(order - CHUNK * q, -1, CHUNK).astype(F32).astype(BF16)
            onehot = jnp.where(iota == rel, one, zero)
            term = jnp.dot(
                rows[:, q * CHUNK : (q + 1) * CHUNK], onehot, preferred_element_type=F32
            )
            picked = term if picked is None else picked + term
        weights = leg[k, :, cols].astype(F32)
        for t in range(2):
            cosine = picked[t * LATPAD : t * LATPAD + LAT]
            sine = picked[(2 + t) * LATPAD : (2 + t) * LATPAD + LAT]
            chosen = jnp.where(sine_part > 0, sine, cosine)
            part[k, t : t + 1, cols] = jnp.sum(chosen * weights, axis=0, keepdims=True)

    def tile(k, carry):
        leg_copy(k).wait()
        window = table[:, pl.ds(pl.multiple_of(k * WIDTH, WIDTH), WIDTH)]
        for n in range(WIDTH // CHUNK):
            pick(k, window, n)
        return carry

    leg_copy(0).wait()
    window = table[:, :WIDTH]
    for n in range(PANEL // CHUNK):
        pick(0, window, n)

    pl.semaphore_wait(barrier, 7 + 14)

    def to(src, dst, send_sem, recv_sem, **peer):
        return pltpu.make_async_remote_copy(
            src_ref=src,
            dst_ref=dst,
            send_sem=send_sem,
            recv_sem=recv_sem,
            device_id=peer,
            device_id_type=mesh_ids,
        )

    sets = (firsts, wides)
    parts = (got1, got)
    lat_copies, far = ([], []), ([], [])
    scale = F32(1.0 / math.sqrt(NLON))

    def send_parts(n):
        for d, peer in enumerate(lats):
            src = part.at[0, :, pl.ds(0, PANEL)] if n == 0 else part.at[peer]
            k = 7 * n + d
            lat_copies[n].append(
                to(src, parts[n].at[j], lat_send.at[k], lat_recv.at[k], lat=peer)
            )
        for copy in lat_copies[n]:
            copy.start()
        parts[n][j] = part[0, :, :PANEL] if n == 0 else part[j]

    def send_far(n):
        for copy in lat_copies[n]:
            copy.wait_recv()
        total = parts[n][0]
        for s in range(1, 8):
            total = total + parts[n][s]
        sets[n][1] = (total * scale).astype(BF16)
        for s, a in enumerate(FARS):
            if a:
                far[n].append(
                    to(
                        sets[n].at[1],
                        sets[n].at[s],
                        far_send.at[5 * n + s],
                        far_recv.at[5 * n + s],
                        tm=tm_of(yh, z - a, core),
                    )
                )
        for copy in far[n]:
            copy.start()

    send_parts(0)
    for n in range(PANEL // CHUNK, WIDTH // CHUNK):
        pick(0, window, n)
    lax.fori_loop(1, 4, tile, 0)
    send_far(0)
    lax.fori_loop(4, 8, tile, 0)
    send_parts(1)

    near, across = ([], []), ([], [])
    for n in range(2):
        for y in range(2):
            for b, at, count in NEARS:
                k = 8 * n + len(across[n])
                here = pl.ds(16 * y + at, count)
                if y or b:
                    near[n].append(
                        to(
                            sets[n].at[pl.ds(0, count)],
                            sets[n].at[here],
                            near_send.at[k],
                            near_recv.at[k],
                            tm=tm_of(yh if y == 0 else 1 - yh, z - b, core),
                        )
                    )
                else:
                    near[n].append(None)
                across[n].append(
                    to(
                        sets[n].at[here],
                        sets[n].at[pl.ds(32 + 16 * y + at, count)],
                        core_send.at[k],
                        core_recv.at[k],
                        tm=other,
                    )
                )

    def send_near(n):
        for copy in far[n]:
            copy.wait_recv()
        for copy in near[n]:
            if copy is not None:
                copy.start()
        across[n][0].start()

    def pass_on(n):
        for copy, onward in zip(near[n][1:], across[n][1:]):
            copy.wait_recv()
            onward.start()

    send_near(0)
    send_far(1)
    pass_on(0)
    for copy in across[0]:
        copy.wait_recv()

    root = i // 8
    lanes = pl.ds(pl.multiple_of((i % 8) * BLOCK, BLOCK), BLOCK)
    row_copies = [
        to(wides.at[:, :, lanes], row_ref, row_send.at[d], row_recv, lat=peer)
        for d, peer in enumerate(lats)
    ]
    here = pltpu.make_async_copy(wides.at[:, :, lanes], row_ref, keep)

    def send_rows():
        for copy in across[1]:
            copy.wait_recv()

        @pl.when(j == root)
        def _():
            for copy in row_copies:
                copy.start()
            here.start()

    def wait_rows():
        @pl.when(j == root)
        def _():
            here.wait()
            for copy in row_copies:
                copy.wait_send()

        @pl.when(j != root)
        def _():
            to(wides.at[:, :, lanes], row_ref, row_send.at[0], row_recv, lat=root).wait_recv()

    ridge = ridge_ref[0]

    def lam_of(degree):
        return ridge * (1.0 + (degree * (degree + 1)).astype(F32) / float(LMAX * (LMAX + 1)))

    lam = lam_of(table[0:1, :PANEL])
    row_id = lax.broadcasted_iota(jnp.int32, (BLOCK, BLOCK), 0)
    col_id = lax.broadcasted_iota(jnp.int32, (BLOCK, BLOCK), 1)
    eye = (row_id == col_id).astype(F32)
    inverse = F32(1.0 / NT)
    first_cols = firsts[...].reshape(NT, PANEL)
    blocks = [first_cols[:, BLOCK * b : BLOCK * (b + 1)] for b in range(4)]
    lams = [lam[:, BLOCK * b : BLOCK * (b + 1)] for b in range(4)]

    total, spd = eye, []
    for b in range(4):
        total = total + contract(blocks[b].astype(F32) * (inverse / lams[b]), blocks[b], LANES)
        spd.append(total)
    eliminate(spd, [eye] * 4, upper, solved, (lambda: send_near(1),))
    pass_on(1)
    spd, rhs = [], []
    for b in range(4):
        if b == 0:
            spd.append(contract(blocks[0], blocks[0], ROWS) * inverse + eye * lams[0])
            rhs.append(blocks[0].astype(F32).T)
        else:
            low = solved[b - 1]
            first = contract(low, blocks[b], PLAIN)
            spd.append(contract(first, first, ROWS) * inverse + eye * lams[b])
            rhs.append(contract(first, low, ROWS))
    eliminate(spd, rhs, upper2, solved2, (send_rows,))
    wait_rows()
    cols = wides[...].reshape(NT, WIDTH)
    rows_own = row_ref[...].reshape(NT, BLOCK)

    @pl.when(i < 4)
    def _():
        out_ref[...] = contract(solved2[jnp.minimum(i, 3)], cols, PLAIN) * inverse

    @pl.when(i >= 4)
    def _():
        low = solved[3]
        first = contract(low, rows_own, PLAIN)
        left = contract(first, low, ROWS)
        own_cols = pl.ds(pl.multiple_of(j * WIDTH, WIDTH), WIDTH)
        lam_cols = lam_of(table[0:1, own_cols])
        row_glob = i * BLOCK + lax.broadcasted_iota(jnp.int32, (BLOCK, WIDTH), 0)
        col_glob = j * WIDTH + lax.broadcasted_iota(jnp.int32, (BLOCK, WIDTH), 1)
        out_ref[...] = contract(left, cols, PLAIN) * inverse + jnp.where(
            row_glob == col_glob, lam_cols, 0.0
        )

    @pl.when(j == 0)
    def _():
        for b in range(4):
            lower = jnp.where(row_id >= col_id, upper2[b].T, 0.0)
            below = contract(rows_own, solved2[b], ((0,), (1,))) * inverse
            out_ref[:, BLOCK * b : BLOCK * (b + 1)] = jnp.where(
                i > b, below, jnp.where(i == b, lower, 0.0)
            )

    sent = lat_copies[0] + lat_copies[1] + far[0] + far[1] + across[0] + across[1]
    for copy in sent + near[0][1:] + near[1][1:]:
        copy.wait_send()


def factored_tile(fields, legendre, window, ridge):
    dma = pltpu.SemaphoreType.DMA
    hbm = pl.BlockSpec(memory_space=pl.ANY)
    vmem = pl.BlockSpec(memory_space=pltpu.VMEM)
    return pl.pallas_call(
        whole_kernel,
        in_specs=[hbm] * 4 + [pl.BlockSpec(memory_space=pltpu.SMEM)],
        out_specs=vmem,
        out_shape=pltpu.VMEM((BLOCK, WIDTH), F32),
        scratch_shapes=[
            pltpu.VMEM((64, 2, PANEL), BF16),
            pltpu.VMEM((64, 2, WIDTH), BF16),
            pltpu.VMEM((64, 2, BLOCK), BF16),
            pltpu.VMEM((LAT, 2, NLON), BF16),
            pltpu.VMEM((2, HALF, DEEP), BF16),
            pltpu.VMEM((8, LAT, WIDTH), BF16),
            pltpu.VMEM((3, 8 * WIDTH), jnp.int32),
            pltpu.VMEM((DEEP // 128, 2 * LAT, 128), F32),
            pltpu.VMEM((4 * LATPAD, DEEP), BF16),
            pltpu.VMEM((8, 2, WIDTH), F32),
            pltpu.VMEM((8, 2, WIDTH), F32),
            pltpu.VMEM((8, 2, PANEL), F32),
            dma((4,)),
            dma((8,)),
            dma((14,)),
            dma((14,)),
            dma((10,)),
            dma((10,)),
            dma((16,)),
            dma((16,)),
            dma((16,)),
            dma((16,)),
            dma((7,)),
            dma(()),
            dma(()),
        ]
        + [pltpu.VMEM((4, BLOCK, BLOCK), F32)] * 4,
        compiler_params=pltpu.CompilerParams(collective_id=0, has_side_effects=True),
        name="factored",
    )(
        jnp.transpose(fields, (1, 0, 2)),
        jnp.asarray(half_basis()),
        legendre,
        window,
        ridge,
    )


def on_device(fields, legendre, order_table, window_start, ridge):
    window = lax.dynamic_slice_in_dim(order_table, window_start[0], legendre.shape[1], 1)
    return factored_tile(fields, legendre, window, ridge)


def solution(mesh):
    placed = (P("tm", "lat", None), P("lat", None), P(), P(), P())
    return jax.shard_map(
        on_device, mesh=mesh, in_specs=placed, out_specs=P("tm", "lat"), check_vma=False
    )
```

```python
import math

import jax
import jax.numpy as jnp
import numpy as np
from jax import lax
from jax.experimental import pallas as pl
from jax.experimental.pallas import tpu as pltpu
from jax.sharding import PartitionSpec as P

NLON = 1440
HALF = NLON // 2
LMAX = 720
NT = 128
PANEL = 512
BLOCK = 128
WIDTH = 1024
LAT = 90
LATPAD = 96
DEEP = 768
CHUNK = 256
F32 = jnp.float32
BF16 = jnp.bfloat16


def half_basis():
    n = np.arange(HALF)[:, None]
    c = np.arange(HALF)[None, :]
    phase = ((n * c) % NLON).astype(np.float32) * np.float32(2.0 * math.pi / NLON)
    basis = np.zeros((2, HALF, DEEP), np.float32)
    basis[0, :, :HALF] = np.cos(phase)
    basis[1, :, :HALF] = np.sin(phase)
    return basis.astype(BF16)


def split(x):
    high = x.astype(BF16)
    return high, (x - high.astype(F32)).astype(BF16)


def contract(left, right, dims):
    def dot(a, b):
        return lax.dot_general(a, b, (dims, ((), ())), preferred_element_type=F32)

    lefts = (left,) if left.dtype == BF16 else split(left)
    rights = (right,) if right.dtype == BF16 else split(right)
    total = dot(lefts[0], rights[0])
    if len(lefts) > 1:
        total = total + dot(lefts[1], rights[0])
    if len(rights) > 1:
        total = total + dot(lefts[0], rights[1])
    return total


ROWS = ((0,), (0,))
LANES = ((1,), (1,))
PLAIN = ((1,), (0,))


def eliminate(spd, rhs, upper_ref, solved_ref, between=(), panel=32):
    count, size = len(spd), BLOCK
    for b in range(count):
        upper_ref[b] = spd[b]
        solved_ref[b] = rhs[b]
    sub = lax.broadcasted_iota(jnp.int32, (8, size), 0)
    pieces = panel // 8
    for p in range(0, size, panel):
        at = [slice(p + 8 * r, p + 8 * r + 8) for r in range(pieces)]
        x = [[upper_ref[b, rows, :] for rows in at] for b in range(count)]
        y = [[solved_ref[b, rows, :] for rows in at] for b in range(count)]
        for g in range(pieces):
            lane = p + 8 * g
            column = [
                [
                    [
                        jnp.broadcast_to(x[b][r][:, lane + m : lane + m + 1], (8, size))
                        for r in range(g, pieces)
                    ]
                    for m in range(8)
                ]
                for b in range(count)
            ]
            scale = [jnp.ones((8, size), F32) for _ in range(count)]
            for m in range(8):
                for b in range(count):
                    c = column[b][m]
                    root = lax.rsqrt(jnp.broadcast_to(c[0][m : m + 1, :], (8, size)))
                    inverse = root * root
                    scale[b] = jnp.where(sub == m, root, scale[b])
                    x_row = jnp.broadcast_to(x[b][g][m : m + 1, :], (8, size))
                    y_row = jnp.broadcast_to(y[b][g][m : m + 1, :], (8, size))
                    u_rows = [
                        jnp.broadcast_to(column[b][later][0][m : m + 1, :], (8, size))
                        for later in range(m + 1, 8)
                    ]
                    for r in range(g, pieces):
                        factor = c[r - g] * inverse
                        if r == g:
                            factor = jnp.where(sub > m, factor, 0.0)
                        for later in range(m + 1, 8):
                            u = column[b][later]
                            u[r - g] = u[r - g] - factor * u_rows[later - m - 1]
                        x[b][r] = x[b][r] - factor * x_row
                        y[b][r] = y[b][r] - factor * y_row
            for b in range(count):
                x[b][g], y[b][g] = x[b][g] * scale[b], y[b][g] * scale[b]
                upper_ref[b, at[g], :] = x[b][g]
                solved_ref[b, at[g], :] = y[b][g]
        if p + panel < size:
            for b in range(count):
                xs, ys = jnp.concatenate(x[b], axis=0), jnp.concatenate(y[b], axis=0)
                below = xs[:, p + panel :]
                upper_ref[b, p + panel :, :] -= contract(below, xs, ROWS)
                solved_ref[b, p + panel :, :] -= contract(below, ys, ROWS)
        if p // panel < len(between):
            between[p // panel]()


FARS = (6, 0, 3, -3, -6)
NEARS = ((0, 0, 5), (1, 5, 5), (-1, 10, 5), (2, 15, 1))


def whole_kernel(
    fields_hbm,
    basis_hbm,
    leg_hbm,
    table_hbm,
    ridge_ref,
    out_ref,
    firsts,
    wides,
    row_ref,
    fields,
    basis,
    leg,
    table,
    spectra,
    rows,
    part,
    got,
    got1,
    load,
    legs,
    lat_send,
    lat_recv,
    far_send,
    far_recv,
    near_send,
    near_recv,
    core_send,
    core_recv,
    row_send,
    row_recv,
    keep,
    upper,
    solved,
    upper2,
    solved2,
):
    i, j = lax.axis_index("tm"), lax.axis_index("lat")
    core, z, yh = i % 2, (i // 2) % 16, i // 32
    mesh_ids = pl.DeviceIdType.MESH

    def tm_of(y_part, z_part, core_part):
        return (y_part * 16 + (z_part + 16) % 16) * 2 + core_part

    lats = [(j + d) % 8 for d in range(1, 8)]
    other = tm_of(yh, z, 1 - core)
    greeted = [tm_of(yh, z + d, core) for d in (3, -3, 6, -6, 1, -1, 2, -2)]
    greeted += [tm_of(1 - yh, z + d, core) for d in (0, 1, -1, 2, -2)]
    greeted += [other]

    loads = [
        pltpu.make_async_copy(fields_hbm, fields, load.at[0]),
        pltpu.make_async_copy(basis_hbm.at[0], basis.at[0], load.at[1]),
        pltpu.make_async_copy(basis_hbm.at[1], basis.at[1], load.at[2]),
        pltpu.make_async_copy(table_hbm, table, load.at[3]),
    ]
    for copy in loads:
        copy.start()

    def leg_copy(k):
        cols = pl.ds(pl.multiple_of(k * WIDTH, WIDTH), WIDTH)
        return pltpu.make_async_copy(leg_hbm.at[:, cols], leg.at[k], legs.at[k])

    for k in range(8):
        leg_copy(k).start()
    barrier = pltpu.get_barrier_semaphore()
    for peer in lats:
        pl.semaphore_signal(barrier, inc=1, device_id={"lat": peer}, device_id_type=mesh_ids)
    for peer in greeted:
        pl.semaphore_signal(barrier, inc=1, device_id={"tm": peer}, device_id_type=mesh_ids)

    loads[0].wait()
    lane = lax.broadcasted_iota(jnp.int32, (1, DEEP), 1)
    sign = jnp.where(lane % 2 == 0, 1.0, -1.0).astype(F32)
    flat = fields[...].reshape(2 * LAT, NLON)
    low, high = flat[:, :HALF], flat[:, HALF:]
    for p in range(2):
        loads[1 + p].wait()
        first = jnp.dot(low, basis[p], preferred_element_type=F32)
        second = jnp.dot(high, basis[p], preferred_element_type=F32)
        both = first + sign * second
        for v in range(DEEP // 128):
            lanes = slice(v * 128, (v + 1) * 128)
            spectra[v] = both[:, lanes]
            for t in range(2):
                at = (2 * p + t) * LATPAD
                rows[at : at + LAT, lanes] = spectra[v, pl.ds(t, LAT, stride=2), :].astype(BF16)

    loads[3].wait()
    iota = lax.broadcasted_iota(jnp.int32, (CHUNK, CHUNK), 0).astype(F32).astype(BF16)
    one, zero = jnp.ones((CHUNK, CHUNK), BF16), jnp.zeros((CHUNK, CHUNK), BF16)

    def pick(k, window, n):
        cols = slice(n * CHUNK, (n + 1) * CHUNK)
        order, sine_part = window[1:2, cols], window[2:3, cols]
        picked = None
        for q in range(DEEP // CHUNK):
            rel = jnp.clip(order - CHUNK * q, -1, CHUNK).astype(F32).astype(BF16)
            onehot = jnp.where(iota == rel, one, zero)
            term = jnp.dot(
                rows[:, q * CHUNK : (q + 1) * CHUNK], onehot, preferred_element_type=F32
            )
            picked = term if picked is None else picked + term
        weights = leg[k, :, cols].astype(F32)
        for t in range(2):
            cosine = picked[t * LATPAD : t * LATPAD + LAT]
            sine = picked[(2 + t) * LATPAD : (2 + t) * LATPAD + LAT]
            chosen = jnp.where(sine_part > 0, sine, cosine)
            part[k, t : t + 1, cols] = jnp.sum(chosen * weights, axis=0, keepdims=True)

    def tile(k, carry):
        leg_copy(k).wait()
        window = table[:, pl.ds(pl.multiple_of(k * WIDTH, WIDTH), WIDTH)]
        for n in range(WIDTH // CHUNK):
            pick(k, window, n)
        return carry

    leg_copy(0).wait()
    window = table[:, :WIDTH]
    for n in range(PANEL // CHUNK):
        pick(0, window, n)

    pl.semaphore_wait(barrier, 7 + 14)

    def to(src, dst, send_sem, recv_sem, **peer):
        return pltpu.make_async_remote_copy(
            src_ref=src,
            dst_ref=dst,
            send_sem=send_sem,
            recv_sem=recv_sem,
            device_id=peer,
            device_id_type=mesh_ids,
        )

    sets = (firsts, wides)
    parts = (got1, got)
    lat_copies, far = ([], []), ([], [])
    scale = F32(1.0 / math.sqrt(NLON))

    def send_parts(n):
        for d, peer in enumerate(lats):
            src = part.at[0, :, pl.ds(0, PANEL)] if n == 0 else part.at[peer]
            k = 7 * n + d
            lat_copies[n].append(
                to(src, parts[n].at[j], lat_send.at[k], lat_recv.at[k], lat=peer)
            )
        for copy in lat_copies[n]:
            copy.start()
        parts[n][j] = part[0, :, :PANEL] if n == 0 else part[j]

    def send_far(n):
        for copy in lat_copies[n]:
            copy.wait_recv()
        total = parts[n][0]
        for s in range(1, 8):
            total = total + parts[n][s]
        sets[n][1] = (total * scale).astype(BF16)
        for s, a in enumerate(FARS):
            if a:
                far[n].append(
                    to(
                        sets[n].at[1],
                        sets[n].at[s],
                        far_send.at[5 * n + s],
                        far_recv.at[5 * n + s],
                        tm=tm_of(yh, z - a, core),
                    )
                )
        for copy in far[n]:
            copy.start()

    send_parts(0)
    for n in range(PANEL // CHUNK, WIDTH // CHUNK):
        pick(0, window, n)
    lax.fori_loop(1, 6, tile, 0)
    send_far(0)
    lax.fori_loop(6, 8, tile, 0)
    send_parts(1)

    near, across = ([], []), ([], [])
    for n in range(2):
        for y in range(2):
            for b, at, count in NEARS:
                k = 8 * n + len(across[n])
                here = pl.ds(16 * y + at, count)
                if y or b:
                    near[n].append(
                        to(
                            sets[n].at[pl.ds(0, count)],
                            sets[n].at[here],
                            near_send.at[k],
                            near_recv.at[k],
                            tm=tm_of(yh if y == 0 else 1 - yh, z - b, core),
                        )
                    )
                else:
                    near[n].append(None)
                across[n].append(
                    to(
                        sets[n].at[here],
                        sets[n].at[pl.ds(32 + 16 * y + at, count)],
                        core_send.at[k],
                        core_recv.at[k],
                        tm=other,
                    )
                )

    def send_near(n):
        for copy in far[n]:
            copy.wait_recv()
        for copy in near[n]:
            if copy is not None:
                copy.start()
        across[n][0].start()

    def pass_on(n):
        for copy, onward in zip(near[n][1:], across[n][1:]):
            copy.wait_recv()
            onward.start()

    send_near(0)
    send_far(1)
    pass_on(0)
    for copy in across[0]:
        copy.wait_recv()
    send_near(1)

    root = i // 8
    lanes = pl.ds(pl.multiple_of((i % 8) * BLOCK, BLOCK), BLOCK)
    row_copies = [
        to(wides.at[:, :, lanes], row_ref, row_send.at[d], row_recv, lat=peer)
        for d, peer in enumerate(lats)
    ]
    here = pltpu.make_async_copy(wides.at[:, :, lanes], row_ref, keep)

    def send_rows():
        for copy in across[1]:
            copy.wait_recv()

        @pl.when(j == root)
        def _():
            for copy in row_copies:
                copy.start()
            here.start()

    def wait_rows():
        @pl.when(j == root)
        def _():
            here.wait()
            for copy in row_copies:
                copy.wait_send()

        @pl.when(j != root)
        def _():
            to(wides.at[:, :, lanes], row_ref, row_send.at[0], row_recv, lat=root).wait_recv()

    ridge = ridge_ref[0]

    def lam_of(degree):
        return ridge * (1.0 + (degree * (degree + 1)).astype(F32) / float(LMAX * (LMAX + 1)))

    lam = lam_of(table[0:1, :PANEL])
    row_id = lax.broadcasted_iota(jnp.int32, (BLOCK, BLOCK), 0)
    col_id = lax.broadcasted_iota(jnp.int32, (BLOCK, BLOCK), 1)
    eye = (row_id == col_id).astype(F32)
    inverse = F32(1.0 / NT)
    first_cols = firsts[...].reshape(NT, PANEL)
    blocks = [first_cols[:, BLOCK * b : BLOCK * (b + 1)] for b in range(4)]
    lams = [lam[:, BLOCK * b : BLOCK * (b + 1)] for b in range(4)]

    total, spd = eye, []
    for b in range(4):
        total = total + contract(blocks[b].astype(F32) * (inverse / lams[b]), blocks[b], LANES)
        spd.append(total)
    eliminate(spd, [eye] * 4, upper, solved, (lambda: None, lambda: None, lambda: pass_on(1)))
    spd, rhs = [], []
    for b in range(4):
        if b == 0:
            spd.append(contract(blocks[0], blocks[0], ROWS) * inverse + eye * lams[0])
            rhs.append(blocks[0].astype(F32).T)
        else:
            low = solved[b - 1]
            first = contract(low, blocks[b], PLAIN)
            spd.append(contract(first, first, ROWS) * inverse + eye * lams[b])
            rhs.append(contract(first, low, ROWS))
    send_rows()
    eliminate(spd, rhs, upper2, solved2)
    wait_rows()
    cols = wides[...].reshape(NT, WIDTH)
    rows_own = row_ref[...].reshape(NT, BLOCK)

    @pl.when(i < 4)
    def _():
        out_ref[...] = contract(solved2[jnp.minimum(i, 3)], cols, PLAIN) * inverse

    @pl.when(i >= 4)
    def _():
        low = solved[3]
        first = contract(low, rows_own, PLAIN)
        left = contract(first, low, ROWS)
        own_cols = pl.ds(pl.multiple_of(j * WIDTH, WIDTH), WIDTH)
        lam_cols = lam_of(table[0:1, own_cols])
        row_glob = i * BLOCK + lax.broadcasted_iota(jnp.int32, (BLOCK, WIDTH), 0)
        col_glob = j * WIDTH + lax.broadcasted_iota(jnp.int32, (BLOCK, WIDTH), 1)
        out_ref[...] = contract(left, cols, PLAIN) * inverse + jnp.where(
            row_glob == col_glob, lam_cols, 0.0
        )

    @pl.when(j == 0)
    def _():
        for b in range(4):
            lower = jnp.where(row_id >= col_id, upper2[b].T, 0.0)
            below = contract(rows_own, solved2[b], ((0,), (1,))) * inverse
            out_ref[:, BLOCK * b : BLOCK * (b + 1)] = jnp.where(
                i > b, below, jnp.where(i == b, lower, 0.0)
            )

    sent = lat_copies[0] + lat_copies[1] + far[0] + far[1] + across[0] + across[1]
    for copy in sent + near[0][1:] + near[1][1:]:
        copy.wait_send()


def factored_tile(fields, legendre, window, ridge):
    dma = pltpu.SemaphoreType.DMA
    hbm = pl.BlockSpec(memory_space=pl.ANY)
    vmem = pl.BlockSpec(memory_space=pltpu.VMEM)
    return pl.pallas_call(
        whole_kernel,
        in_specs=[hbm] * 4 + [pl.BlockSpec(memory_space=pltpu.SMEM)],
        out_specs=vmem,
        out_shape=pltpu.VMEM((BLOCK, WIDTH), F32),
        scratch_shapes=[
            pltpu.VMEM((64, 2, PANEL), BF16),
            pltpu.VMEM((64, 2, WIDTH), BF16),
            pltpu.VMEM((64, 2, BLOCK), BF16),
            pltpu.VMEM((LAT, 2, NLON), BF16),
            pltpu.VMEM((2, HALF, DEEP), BF16),
            pltpu.VMEM((8, LAT, WIDTH), BF16),
            pltpu.VMEM((3, 8 * WIDTH), jnp.int32),
            pltpu.VMEM((DEEP // 128, 2 * LAT, 128), F32),
            pltpu.VMEM((4 * LATPAD, DEEP), BF16),
            pltpu.VMEM((8, 2, WIDTH), F32),
            pltpu.VMEM((8, 2, WIDTH), F32),
            pltpu.VMEM((8, 2, PANEL), F32),
            dma((4,)),
            dma((8,)),
            dma((14,)),
            dma((14,)),
            dma((10,)),
            dma((10,)),
            dma((16,)),
            dma((16,)),
            dma((16,)),
            dma((16,)),
            dma((7,)),
            dma(()),
            dma(()),
        ]
        + [pltpu.VMEM((4, BLOCK, BLOCK), F32)] * 4,
        compiler_params=pltpu.CompilerParams(collective_id=0, has_side_effects=True),
        name="factored",
    )(
        jnp.transpose(fields, (1, 0, 2)),
        jnp.asarray(half_basis()),
        legendre,
        window,
        ridge,
    )


def on_device(fields, legendre, order_table, window_start, ridge):
    window = lax.dynamic_slice_in_dim(order_table, window_start[0], legendre.shape[1], 1)
    return factored_tile(fields, legendre, window, ridge)


def solution(mesh):
    placed = (P("tm", "lat", None), P("lat", None), P(), P(), P())
    return jax.shard_map(
        on_device, mesh=mesh, in_specs=placed, out_specs=P("tm", "lat"), check_vma=False
    )
```
